128 devices in a mesh: dev: 128 (over x, y, z, core).
Axes of the slice: x: 4, y: 4, z: 4, core: 2. Of those that a mesh axis runs over, the one named last changes fastest.
Arguments:
- params: float32 [9, 131072], P(None, 'dev')
- moment: float32 [9, 131072], P(None, 'dev'), may hold values from -3 to 3
- second: float32 [9, 131072], P(None, 'dev'), may hold values from 0.05 to 1
- fetch_ids: int32 [128, 128, 8], P('dev'), may hold values from 0 to 1023
- seg_ids: int32 [512, 256], P('dev'), may hold values from 0 to 1023
- seg_count: int32 [512], P('dev'), may hold values from 1 to 256, 98304 in all
- seg_perm: int32 [512], replicated, may hold values from 0 to 511, as said below
- target: float32 [128, 3, 256], P('dev'), may hold values from 0 to 1
Outputs:
- image: float32 [128, 3, 256], P('dev')
- new_params: float32 [9, 131072], P(None, 'dev')
- new_moment: float32 [9, 131072], P(None, 'dev')
- new_second: float32 [9, 131072], P(None, 'dev')
The draws below stay inside these ranges and needn't reach their ends.
Inputs may be any that keep to these rules, and one draw needn't show every extreme that they name: `seg_count`: segments that exceed their count hold unused slots; some segment is full. `seg_perm`: each number appears once.
All inputs are finite; a program needn't handle non-finite values. No bound on the sum of `seg_count` on one device may be relied on, other than what follows from the above.
Results may differ from the reference program's by a relative error of at most 0.0003.
Values sent between devices are 32-bit elements; how exact they have to be, the bound alone decides.
A program may use at most 192 MiB of HBM per device.

```python
import math
import jax
import jax.numpy as jnp
import numpy as np
from jax import lax

PARAMS = 9
TILE_PIX = 256
TILES_X = 8
KSEG = 4
SEG_LEN = 256
SPL_DEV = 1024
CAP = 8
SEGS_DEV = 4
SPLATS = 131072
SLOTS = 1024
SEGMENTS = 512
TILES = 128
N_DEV = 128


def permute_rows(key, rows, width):
    return jax.vmap(lambda one: jax.random.permutation(one, width))(jax.random.split(key, rows)).astype(jnp.int32)


def layout(key):
    base = jax.random.fold_in(key, 101)
    seg_perm = jax.random.permutation(jax.random.fold_in(base, 1), SEGMENTS).astype(jnp.int32)
    orders = permute_rows(jax.random.fold_in(base, 2), N_DEV, SPL_DEV)
    request = jnp.arange(N_DEV, dtype=jnp.int32)[:, None, None] * CAP + jnp.arange(CAP, dtype=jnp.int32)[None, None, :]
    request = jnp.broadcast_to(request, (N_DEV, N_DEV, CAP)) % SPL_DEV
    owners = jnp.broadcast_to(jnp.arange(N_DEV, dtype=jnp.int32)[None, :, None], (N_DEV, N_DEV, CAP))
    fresh = orders[owners, request]
    repeat = jax.random.randint(jax.random.fold_in(base, 3), (N_DEV, N_DEV, CAP), 0, 8) == 0
    partner = jax.random.randint(jax.random.fold_in(base, 4), (N_DEV, N_DEV, CAP), 0, CAP).astype(jnp.int32)
    within = jnp.broadcast_to(jnp.arange(CAP, dtype=jnp.int32), (N_DEV, N_DEV, CAP))
    source = jnp.where(repeat, partner, within)
    fetch_ids = jnp.take_along_axis(fresh, source, axis=2).astype(jnp.int32)
    home_base = (permute_rows(jax.random.fold_in(base, 5), N_DEV, SLOTS) % SEGS_DEV).reshape(N_DEV, N_DEV, CAP)
    home = jnp.take_along_axis(home_base, source, axis=2).reshape(N_DEV, SLOTS).astype(jnp.int32)
    tiebreak = permute_rows(jax.random.fold_in(base, 6), N_DEV, SLOTS)
    sorted_slots = jnp.argsort(home * SLOTS + tiebreak, axis=1).astype(jnp.int32)
    counts = jnp.sum((home[:, None, :] == jnp.arange(SEGS_DEV, dtype=jnp.int32)[None, :, None]).astype(jnp.int32), axis=2).astype(jnp.int32)
    starts = jnp.cumsum(counts, axis=1).astype(jnp.int32) - counts
    picks = jax.random.randint(jax.random.fold_in(base, 7), (N_DEV, SEGS_DEV, SEG_LEN), 0, 1 << 30).astype(jnp.int32)
    position = starts[:, :, None] + picks % jnp.maximum(counts, 1)[:, :, None]
    position = jnp.minimum(position, SLOTS - 1).reshape(N_DEV, SEGS_DEV * SEG_LEN)
    chosen = jnp.take_along_axis(sorted_slots, position, axis=1).reshape(N_DEV, SEGS_DEV, SEG_LEN)
    seg_ids = jnp.where(counts[:, :, None] > 0, chosen, picks % SLOTS).reshape(SEGMENTS, SEG_LEN).astype(jnp.int32)
    device_base = jnp.arange(N_DEV, dtype=jnp.int32)[:, None] * SEGS_DEV
    slot_tile = seg_perm[device_base + home] // KSEG
    global_ids = (jnp.arange(N_DEV, dtype=jnp.int32)[None, :, None] * SPL_DEV + fetch_ids).reshape(N_DEV, SLOTS)
    score = jnp.arange(N_DEV, dtype=jnp.int32)[:, None] * SLOTS + jnp.arange(SLOTS, dtype=jnp.int32)[None, :]
    user = jnp.full((SPLATS,), -1, jnp.int32).at[global_ids.reshape(-1)].max(score.reshape(-1))
    spare = jax.random.randint(jax.random.fold_in(base, 8), (SPLATS,), 0, TILES).astype(jnp.int32)
    splat_tile = jnp.where(user >= 0, slot_tile.reshape(-1)[jnp.maximum(user, 0)], spare).astype(jnp.int32)
    return (fetch_ids, seg_ids, seg_perm, splat_tile)


def draw_fetch_ids(key, part):
    return layout(key)[0]


def draw_seg_ids(key, part):
    return layout(key)[1]


def draw_seg_perm(key, part):
    return layout(key)[2]


def draw_params(key, part):
    splat_tile = layout(key)[3]
    keys = jax.random.split(jax.random.fold_in(key, 11), 10)
    count = SPLATS
    scales = jax.random.uniform(keys[2], (2, count), jnp.float32, 1.5, 3.0)
    sigma_x = jnp.exp(-scales[0])
    sigma_y = jnp.exp(-scales[1])
    corner_x = (splat_tile % TILES_X).astype(jnp.float32)
    corner_y = (splat_tile // TILES_X).astype(jnp.float32)
    centre_x = corner_x + jax.random.uniform(keys[0], (count,), jnp.float32, 0.0, 1.0) + 2.0 * sigma_x * jax.random.uniform(keys[6], (count,), jnp.float32, -1.0, 1.0)
    centre_y = corner_y + jax.random.uniform(keys[1], (count,), jnp.float32, 0.0, 1.0) + 2.0 * sigma_y * jax.random.uniform(keys[7], (count,), jnp.float32, -1.0, 1.0)
    opaque = jax.random.uniform(keys[8], (count,), jnp.float32, 0.0, 1.0) < min(1.0, 16.0 / SEG_LEN)
    weak = jax.random.uniform(keys[9], (count,), jnp.float32, -8.0, -1.0)
    tilt = jax.random.normal(keys[3], (1, count), jnp.float32)
    strong = jax.random.uniform(keys[4], (count,), jnp.float32, 1.0, 4.0)
    colours = jax.random.uniform(keys[5], (3, count), jnp.float32, 0.0, 1.0)
    opacity = jnp.where(opaque, strong, weak)[None, :]
    return jnp.concatenate([centre_x[None, :], centre_y[None, :], scales, tilt, opacity, colours], axis=0)


def block_levels(stream_key, extent, pieces, smallest, top_value):
    level = 1.0
    for dim, blocks in pieces:
        steps = jax.random.uniform(jax.random.fold_in(jax.random.fold_in(stream_key, 6), dim), (blocks,), jnp.float32, smallest / len(pieces), top_value / len(pieces))
        level = level * jnp.repeat(jnp.exp(steps), extent[dim] // blocks).reshape((-1,) + (1,) * (len(extent) - 1 - dim))
    return level


def length_profile(amount, total, reach, slope):
    weights = [(1 << 20) // math.isqrt(standing ** slope) + 1 for standing in range(2, amount + 1)]
    surplus, given = total - reach - (amount - 1), [1] * (amount - 1)
    while surplus > 0:
        free = [i for i in range(amount - 1) if given[i] < reach]
        mass, remaining = sum([weights[i] for i in free]), surplus
        for i in free:
            more = min(reach - given[i], max(1, remaining * weights[i] // mass), surplus)
            given[i] = given[i] + more
            surplus = surplus - more
    return np.array([reach] + given)


def ragged(own_key, number_of, total, limit, skew):
    if number_of == 2:
        one = jax.random.randint(own_key, (), max(1, total - limit), min(limit, total - 1) + 1)
        return jnp.stack([one, total - one])
    lengths = jnp.asarray(length_profile(number_of, total, limit, skew), jnp.int32)
    couples = (number_of - 1) // 2
    giver, receiver = lengths[1:1 + 2 * couples:2], lengths[2:2 + 2 * couples:2]
    room = jnp.minimum(giver - 1, limit - receiver)
    moved = jax.random.randint(jax.random.fold_in(own_key, 1), (couples,), 0, 1 << 20) % (room + 1)
    lengths = lengths.at[1:1 + 2 * couples:2].set(giver - moved).at[2:2 + 2 * couples:2].set(receiver + moved)
    return lengths[jax.random.permutation(jax.random.fold_in(own_key, 2), number_of)]


def gaussian(key, extent, spread, limit, cuts=(), kind=jnp.bfloat16):
    gain = block_levels(key, extent, cuts, -0.22, 0.18) if cuts else 1.0
    array = jax.random.normal(key, extent, jnp.float32) * spread * gain
    return jnp.minimum(jnp.maximum(array, -limit), limit).astype(kind)


def setup_inputs(seed: int = 0) -> dict:
    key_list = jax.random.split(jax.random.key(seed), 9)
    params = draw_params(jax.random.fold_in(key_list[8], 71), 0)
    moment = gaussian(key_list[1], (PARAMS, SPLATS), 0.5, 3.0, ((1, 128),), jnp.float32)
    second = jnp.clip(jnp.exp(math.log(1.0) - 2.9957323 * jax.random.uniform(key_list[2], (PARAMS, SPLATS), jnp.float32) ** block_levels(key_list[2], (PARAMS, SPLATS), ((1, 128),), -0.2, 0.2)), 0.05, 1.0)
    fetch_ids = draw_fetch_ids(jax.random.fold_in(key_list[8], 71), 0)
    seg_ids = draw_seg_ids(jax.random.fold_in(key_list[8], 71), 0)
    seg_count = ragged(key_list[5], SEGMENTS, SEGMENTS * SEG_LEN * 3 // 4, SEG_LEN, 2).astype(jnp.int32)
    seg_perm = draw_seg_perm(jax.random.fold_in(key_list[8], 71), 0)
    target = jnp.clip(1.0 * jax.random.uniform(key_list[7], (TILES, 3, TILE_PIX), jnp.float32) ** block_levels(key_list[7], (TILES, 3, TILE_PIX), ((0, 128),), -0.2, 0.2), 0.0, 1.0)
    return {"params": params, "moment": moment, "second": second, "fetch_ids": fetch_ids, "seg_ids": seg_ids, "seg_count": seg_count, "seg_perm": seg_perm, "target": target}


def segment(par, count, tile):
    span = par.shape[1]
    pidx = jnp.arange(256, dtype=jnp.int32)
    fine_x = ((pidx % 16).astype(jnp.float32) + 0.5) / 16.0
    fine_y = ((pidx // 16).astype(jnp.float32) + 0.5) / 16.0
    pos_x = (tile % TILES_X).astype(jnp.float32) + fine_x
    pos_y = (tile // TILES_X).astype(jnp.float32) + fine_y
    live = (jnp.arange(span, dtype=jnp.int32) < count).astype(jnp.float32)
    delta_x = pos_x[None, :] - par[0][:, None]
    delta_y = pos_y[None, :] - par[1][:, None]
    scale_a = jnp.exp(par[2])
    scale_c = jnp.exp(par[3])
    cross = 0.8 * jnp.tanh(par[4]) * scale_a * scale_c
    power = -0.5 * ((scale_a * scale_a)[:, None] * delta_x * delta_x + 2.0 * cross[:, None] * delta_x * delta_y + (scale_c * scale_c)[:, None] * delta_y * delta_y)
    alpha = (0.95 * jax.nn.sigmoid(par[5]) * live)[:, None] * jnp.exp(power)
    logt = jnp.log1p(-alpha)
    earlier = jnp.cumsum(logt, axis=0) - logt
    weight = jnp.exp(earlier) * alpha
    colour = jnp.dot(par[6:9], weight, precision=lax.Precision.HIGHEST)
    return (colour, lax.optimization_barrier(jnp.sum(logt, axis=0)))

def reference(params, moment, second, fetch_ids, seg_ids, seg_count, seg_perm, target):
    slots = jnp.arange(SEGMENTS, dtype=jnp.int32)
    requester = slots // SEGS_DEV
    owner = seg_ids // CAP
    within = seg_ids % CAP
    local = fetch_ids[requester[:, None], owner, within]
    global_ids = owner * SPL_DEV + local
    tiles = seg_perm // KSEG
    order = jnp.zeros((SEGMENTS,), jnp.int32).at[seg_perm].set(slots)

    def render(values):

        def one(args):
            ids, count, tile = args
            return segment(jnp.take(values, ids, axis=1), count, tile)
        colours, logs = lax.map(jax.checkpoint(one), (global_ids, seg_count, tiles))
        colours = colours[order].reshape(TILES, KSEG, 3, TILE_PIX)
        logs = logs[order].reshape(TILES, KSEG, TILE_PIX)
        before = jnp.cumsum(logs, axis=1) - logs
        return lax.optimization_barrier(jnp.sum(jnp.exp(before)[:, :, None, :] * colours, axis=1))
    image, back = jax.vjp(render, params)
    grad, = back(image - target)
    new_moment = 0.9 * moment + 0.1 * grad
    new_second = 0.99 * second + 0.01 * grad * grad
    new_params = params - 0.05 * new_moment / (jnp.sqrt(new_second) + 1e-08)
    return (image, new_params, new_moment, new_second)
```

```python
import jax
import jax.numpy as jnp
from jax import lax
from jax.sharding import PartitionSpec as P

TILES_X = 8
KSEG = 4


def segment(par, count, tile):
    span = par.shape[1]
    pidx = jnp.arange(256, dtype=jnp.int32)
    fine_x = ((pidx % 16).astype(jnp.float32) + 0.5) / 16.0
    fine_y = ((pidx // 16).astype(jnp.float32) + 0.5) / 16.0
    pos_x = (tile % TILES_X).astype(jnp.float32) + fine_x
    pos_y = (tile // TILES_X).astype(jnp.float32) + fine_y
    steps = jnp.arange(span, dtype=jnp.int32)
    live = (steps < count).astype(jnp.float32)
    delta_x = pos_x[None, :] - par[0][:, None]
    delta_y = pos_y[None, :] - par[1][:, None]
    scale_a = jnp.exp(par[2])
    scale_c = jnp.exp(par[3])
    cross = 0.8 * jnp.tanh(par[4]) * scale_a * scale_c
    power = -0.5 * (
        (scale_a * scale_a)[:, None] * delta_x * delta_x
        + 2.0 * cross[:, None] * delta_x * delta_y
        + (scale_c * scale_c)[:, None] * delta_y * delta_y
    )
    alpha = (0.95 * jax.nn.sigmoid(par[5]) * live)[:, None] * jnp.exp(power)
    logt = jnp.log1p(-alpha)
    lower = (steps[:, None] > steps[None, :]).astype(jnp.float32)
    earlier = jnp.dot(lower, logt, precision=lax.Precision.HIGHEST)
    weight = jnp.exp(earlier) * alpha
    colour = jnp.dot(par[6:9], weight, precision=lax.Precision.HIGHEST)
    return (colour, jnp.sum(logt, axis=0))


def per_device(params, moment, second, fetch_ids, seg_ids, seg_count, seg_perm, target):
    ndev = lax.axis_size("dev")
    me = lax.axis_index("dev")
    nparam, owned = params.shape
    segs, span = seg_ids.shape
    tiles_dev = target.shape[0]
    pixels = target.shape[2]
    wanted = fetch_ids[0]
    cap = wanted.shape[1]
    received = lax.all_to_all(wanted, "dev", split_axis=0, concat_axis=0, tiled=True)
    buckets = jnp.take(params, received, axis=1)
    arrived = lax.all_to_all(buckets, "dev", split_axis=1, concat_axis=1, tiled=True)
    buffer = arrived.reshape(nparam, ndev * cap)
    first = me * segs
    own_perm = lax.dynamic_slice_in_dim(seg_perm, first, segs, 0)
    own_tile = own_perm // KSEG
    own_rank = own_perm % KSEG
    gathered_par = jnp.moveaxis(jnp.take(buffer, seg_ids, axis=1), 1, 0)

    def partials(values):
        return jax.vmap(segment)(values, seg_count, own_tile)

    (colours, logs), back = jax.vjp(partials, gathered_par)
    all_colours, all_logs, all_target = (
        lax.all_gather(colours, "dev", axis=0, tiled=True),
        lax.all_gather(logs, "dev", axis=0, tiled=True),
        lax.all_gather(target, "dev", axis=0, tiled=True),
    )
    total = all_logs.shape[0]
    ntiles = all_target.shape[0]
    tile_all = seg_perm // KSEG
    rank_all = seg_perm % KSEG
    same = tile_all[:, None] == tile_all[None, :]
    before = (same & (rank_all[None, :] < rank_all[:, None])).astype(jnp.float32)
    prefix = jnp.exp(jnp.dot(before, all_logs, precision=lax.Precision.HIGHEST))
    contrib = (prefix[:, None, :] * all_colours).reshape(total, 3 * pixels)
    onehot = (jnp.arange(ntiles, dtype=jnp.int32)[:, None] == tile_all[None, :]).astype(jnp.float32)
    image = jnp.dot(onehot, contrib, precision=lax.Precision.HIGHEST)
    misfit = image - all_target.reshape(ntiles, 3 * pixels)
    later = (
        (own_tile[:, None] == tile_all[None, :]) & (rank_all[None, :] > own_rank[:, None])
    ).astype(jnp.float32)
    behind = jnp.dot(later, contrib, precision=lax.Precision.HIGHEST).reshape(segs, 3, pixels)
    picker = (own_tile[:, None] == jnp.arange(ntiles, dtype=jnp.int32)[None, :]).astype(jnp.float32)
    error = jnp.dot(picker, misfit, precision=lax.Precision.HIGHEST).reshape(segs, 3, pixels)
    own_prefix = lax.dynamic_slice_in_dim(prefix, first, segs, 0)
    d_colour = own_prefix[:, None, :] * error
    d_log = jnp.sum(error * behind, axis=1)
    (d_par,) = back((d_colour, d_log))
    slot_grad = (
        jnp.zeros((nparam, ndev * cap), jnp.float32)
        .at[:, seg_ids.reshape(-1)]
        .add(jnp.moveaxis(d_par, 1, 0).reshape(nparam, segs * span))
    )
    returned = lax.all_to_all(
        slot_grad.reshape(nparam, ndev, cap), "dev", split_axis=1, concat_axis=1, tiled=True
    )
    grad = (
        jnp.zeros((nparam, owned), jnp.float32)
        .at[:, received.reshape(-1)]
        .add(returned.reshape(nparam, ndev * cap))
    )
    new_moment = 0.9 * moment + 0.1 * grad
    new_second = 0.99 * second + 0.01 * grad * grad
    new_params = params - 0.05 * new_moment / (jnp.sqrt(new_second) + 1e-08)
    my_image = lax.dynamic_slice_in_dim(image, me * tiles_dev, tiles_dev, 0).reshape(
        tiles_dev, 3, pixels
    )
    return (my_image, new_params, new_moment, new_second)


def solution(mesh):
    placed = (
        P(None, "dev"),
        P(None, "dev"),
        P(None, "dev"),
        P("dev", None, None),
        P("dev", None),
        P("dev"),
        P(),
        P("dev", None, None),
    )
    return jax.shard_map(
        per_device,
        mesh=mesh,
        in_specs=placed,
        out_specs=(P("dev", None, None), P(None, "dev"), P(None, "dev"), P(None, "dev")),
        check_vma=False,
    )
```

```python
import jax
import jax.numpy as jnp
from jax import lax
from jax.experimental import pallas as pl
from jax.experimental.pallas import tpu as pltpu
from jax.sharding import PartitionSpec as P

F32, BF16, I32 = jnp.float32, jnp.bfloat16, jnp.int32
MESH = pl.DeviceIdType.MESH
N = 128
SEGS = 4
SPAN = 256
PIX = 256
CHUNK = 32
CHUNKS = PIX // CHUNK
CAP = 8


def iota(shape, axis):
    return lax.broadcasted_iota(I32, shape, axis)


def onehot(cond):
    return jnp.where(cond, 1.0, 0.0).astype(BF16)


def mm(a, b):
    return jnp.dot(a, b, preferred_element_type=F32)


def split2(x):
    hi = x.astype(BF16)
    lo = (x - hi.astype(F32)).astype(BF16)
    return hi, lo


def split3(x):
    hi = x.astype(BF16)
    rest = x - hi.astype(F32)
    mid = rest.astype(BF16)
    lo = (rest - mid.astype(F32)).astype(BF16)
    return hi, mid, lo


def exact_rows(x, sel):
    n = x.shape[0]
    pad = -n % 16
    if pad:
        x = jnp.concatenate([x, jnp.zeros((pad, x.shape[1]), F32)], axis=0)
    out = mm(jnp.concatenate(split3(x), axis=0), sel)
    m = n + pad
    return (out[:n] + out[m : m + n]) + out[2 * m : 2 * m + n]


def pick(table, sel, high):
    got = exact_rows(table, sel)
    main = jnp.zeros((8, got.shape[1]), F32)
    for h in range(8):
        main = main + jnp.where(high == h, got[8 * h : 8 * h + 8], 0.0)
    last = jnp.where(iota((8, got.shape[1]), 0) == high, got[64:72], 0.0)
    return main, jnp.sum(last, axis=0, keepdims=True)


def spread(main, last, high, sel):
    rows = [jnp.where(high == h, main, 0.0) for h in range(8)]
    rows.append(jnp.where(iota(main.shape, 0) == high, last, 0.0))
    rows.append(jnp.zeros_like(main))
    x = jnp.concatenate(rows, axis=0)
    out = mm(jnp.concatenate(split2(x), axis=0), sel)
    return out[:72] + out[80:152]


def pad_rows(x):
    return jnp.concatenate([x, jnp.zeros((N - x.shape[0], x.shape[1]), F32)], axis=0)


def kernel(
    count_ref, perm_ref, par_ref, mom_ref, sec_ref, fetch_ref, ids_ref, permv_ref, tgt_ref,
    img_ref, npar_ref, nmom_ref, nsec_ref,
    send_buf, recv_buf, e_ref, et_ref, o_ref, ot_ref, ohj_ref, rows_ref, f_ref, q_ref,
    a_ref, w_ref, hi_ref, lo_ref, x_ref, dp_ref, dpl_ref,
    send_sem, recv_sem,
):
    me = lax.axis_index("dev")
    barrier = pltpu.get_barrier_semaphore()

    def greet(i, _):
        pl.semaphore_signal(
            barrier, inc=1, device_id=(lax.rem(me + i, N),), device_id_type=MESH
        )
        return 0

    lax.fori_loop(1, N, greet, 0)

    def send(r):
        def one(i, _):
            to = lax.rem(me + i, N)
            pltpu.make_async_remote_copy(
                src_ref=send_buf.at[r, pl.ds(to, 1)],
                dst_ref=recv_buf.at[r, pl.ds(me, 1)],
                send_sem=send_sem.at[r],
                recv_sem=recv_sem.at[r],
                device_id=(to,),
                device_id_type=MESH,
            ).start()
            return 0

        lax.fori_loop(1, N, one, 0)
        pltpu.make_async_copy(
            send_buf.at[r, pl.ds(me, 1)], recv_buf.at[r, pl.ds(me, 1)], recv_sem.at[r]
        ).start()

    def receive(r):
        pltpu.make_async_copy(send_buf.at[r], recv_buf.at[r], recv_sem.at[r]).wait()
        return recv_buf[r]

    send_buf[0] = pad_rows(fetch_ref[...].astype(F32)).T
    pl.semaphore_wait(barrier, N - 1)
    send(0)

    ids = [ids_ref[s : s + 1, :] for s in range(SEGS)]
    for s in range(SEGS):
        for h in range(2):
            row = jnp.broadcast_to(ids[s][:, h * N : (h + 1) * N] // CAP, (N, N))
            at = (2 * s + h) * N
            sel = jnp.where(iota((N, N), 0) == row, 1.0, 0.0)
            et_ref[:, at : at + N] = sel.astype(BF16)
            e_ref[at : at + N, :] = sel.T.astype(BF16)
    slot = jnp.concatenate(ids, axis=1) % CAP
    table = [par_ref[0:8, c * N : (c + 1) * N] for c in range(8)]
    table += [par_ref[8:9, c * N : (c + 1) * N] for c in range(8)]
    table = jnp.concatenate(table, axis=0)

    got = receive(0).astype(I32)
    wanted = got.astype(F32).T[0:8].astype(I32)
    wanted = jnp.concatenate([wanted[k : k + 1] for k in range(CAP)], axis=1)
    high = wanted // N
    low = wanted % N
    oht = onehot(iota((N, CAP * N), 0) == low)
    main, last = pick(table, oht, high)
    out = [main[:, k * N : (k + 1) * N] for k in range(CAP)]
    out += [last[:, k * N : (k + 1) * N] for k in range(CAP)]
    send_buf[1] = pad_rows(jnp.concatenate(out, axis=0)).T
    send(1)

    lane = iota((N, N), 1)
    for k in range(CAP):
        ohj_ref[k * N : (k + 1) * N, :] = onehot(got[:, k : k + 1] % N == lane)
    nat = permv_ref[...]
    nat = jnp.concatenate([nat // SEGS, nat % SEGS], axis=0).astype(F32).astype(BF16)
    col = iota((N, SEGS * N), 1)
    deal = mm(nat_pad(nat), onehot(iota((N, SEGS * N), 0) == 4 * (col % 32) + col // N))
    quarter = (iota((1, SEGS * N), 1) % N) // 32
    code = jnp.zeros((1, SEGS * N), F32)
    for a in range(4):
        code = code + jnp.where(
            quarter == a, deal[a : a + 1] + N * deal[4 + a : 5 + a], 0.0
        )
    for b in range(4):
        piece = jnp.broadcast_to(code[:, b * N : (b + 1) * N].astype(I32), (N, N))
        for k in range(4):
            sel = jnp.where(iota((N, N), 0) + k * N == piece, 1.0, 0.0)
            o_ref[k * N : (k + 1) * N, b * N : (b + 1) * N] = sel.astype(BF16)
            ot_ref[b * N : (b + 1) * N, k * N : (k + 1) * N] = sel.T.astype(BF16)
    tgt = []
    for h in range(2):
        tgt += [tgt_ref[ch, :, h * N : (h + 1) * N] for ch in range(3)]
        tgt.append(jnp.zeros((1, N), F32))
    tgt = jnp.concatenate([jnp.zeros((32, N), F32)] + tgt, axis=0)
    f_ref[...] = pad_rows(tgt).T

    arrived = receive(1).T
    main, last = pick(arrived[0:72], et_ref[...], slot)
    scale = jnp.exp(main)
    bend = jnp.tanh(main)
    gate = jax.nn.sigmoid(main)
    sa, sc = scale[2:3], scale[3:4]
    th, sg = bend[4:5], gate[5:6]
    cross = 0.8 * th * sa * sc
    step = iota((1, SPAN), 1)
    live = jnp.concatenate(
        [jnp.where(step < count_ref[s], 1.0, 0.0) for s in range(SEGS)], axis=1
    )
    rows = [
        main[0:1], main[1:2], -0.5 * (sa * sa), -cross, -0.5 * (sc * sc), 0.95 * sg * live,
        main[6:7], main[7:8], last, 0.8 * (1.0 - th * th) * sa * sc, 1.0 - sg,
    ]
    for s in range(SEGS):
        for i, row in enumerate(rows):
            rows_ref[s, i : i + 1, :] = row[:, s * SPAN : (s + 1) * SPAN]

    def tile_of(s):
        tile = perm_ref[me * SEGS + s] // SEGS
        return (tile % 8).astype(F32), (tile // 8).astype(F32)

    def row(s, i):
        return rows_ref[s, i : i + 1, :]

    fine_x = (iota((16, SPAN), 0).astype(F32) + 0.5) / 16.0

    def delta_x(s):
        return (tile_of(s)[0] + fine_x) - row(s, 0)

    def delta_y(s, line):
        at = tile_of(s)[1] + (line.astype(F32) + 0.5) / 16.0
        return at - row(s, 1)

    def twice(x):
        return jnp.concatenate([x, x], axis=0)

    def lines(s, c):
        return jnp.concatenate(
            [jnp.broadcast_to(delta_y(s, 2 * c + i), (16, SPAN)) for i in range(2)], axis=0
        )

    def place(s, c):
        return pl.ds(pl.multiple_of(s * PIX + c * CHUNK, CHUNK), CHUNK)

    lane32 = iota((CHUNK, N), 1)

    def forward_a(s, _):
        dx = delta_x(s)
        t1 = twice(row(s, 2) * dx * dx)
        t2 = twice(row(s, 3) * dx)

        def one(c, _):
            dy = lines(s, c)
            alpha = row(s, 5) * jnp.exp(t1 + dy * (t2 + row(s, 4) * dy))
            logt = jnp.log(1.0 - alpha)
            at = place(s, c)
            a_ref[at, :] = alpha
            hi, lo = split2(logt)
            hi_ref[at, :] = hi
            lo_ref[at, :] = lo
            total = jnp.sum(logt, axis=1, keepdims=True)
            q = pl.ds(pl.multiple_of(lax.rem(c, 4) * CHUNK, CHUNK), CHUNK)
            f_ref[q, :] = jnp.where(
                lane32 == 8 * s + 4 * (c // 4) + 3, total, f_ref[q, :]
            )
            return 0

        return lax.fori_loop(0, CHUNKS, one, 0)

    lax.fori_loop(0, SEGS, forward_a, 0)

    tri = iota((SPAN, SPAN), 0) < iota((SPAN, SPAN), 1)
    earlier = onehot(tri)

    def sums(s, _):
        at = pl.ds(pl.multiple_of(s * PIX, PIX), PIX)
        x_ref[at, :] = mm(hi_ref[at, :], earlier) + mm(lo_ref[at, :], earlier)
        return 0

    lax.fori_loop(0, SEGS, sums, 0)

    def forward_b(s, _):
        def one(c, _):
            at = place(s, c)
            alpha = a_ref[at, :]
            weight = jnp.exp(x_ref[at, :]) * alpha
            w_ref[at, :] = weight
            a_ref[at, :] = alpha / (1.0 - alpha)
            q = pl.ds(pl.multiple_of(lax.rem(c, 4) * CHUNK, CHUNK), CHUNK)
            kept = f_ref[q, :]
            for ch in range(3):
                total = jnp.sum(weight * row(s, 6 + ch), axis=1, keepdims=True)
                kept = jnp.where(lane32 == 8 * s + 4 * (c // 4) + ch, total, kept)
            f_ref[q, :] = kept
            return 0

        return lax.fori_loop(0, CHUNKS, one, 0)

    lax.fori_loop(0, SEGS, forward_b, 0)

    send_buf[2] = f_ref[...]
    send(2)
    seen = receive(2).T
    by_seg = jnp.concatenate([seen[8 * s : 8 * s + 8] for s in range(SEGS)], axis=1)
    target = seen[32:40]
    by_tile = exact_rows(by_seg, ot_ref[...])
    sub = iota((8, N), 0) % 4
    colour = sub < 3
    before = jnp.zeros((8, N), F32)
    image = jnp.zeros((8, N), F32)
    terms = []
    for k in range(4):
        part = by_tile[:, k * N : (k + 1) * N]
        through = jnp.exp(before)
        contrib = jnp.where(colour, through * part, 0.0)
        terms.append((through, contrib))
        image = image + contrib
        log = jnp.where(colour, 0.0, part)
        log = log + pltpu.roll(log, 7, 0)
        before = before + (log + pltpu.roll(log, 6, 0))
    error = jnp.where(colour, image - target, 0.0)
    behind = jnp.zeros((8, N), F32)
    back = [None] * 4
    for k in (3, 2, 1, 0):
        through, contrib = terms[k]
        z = error * behind
        z = pltpu.roll(z, 1, 0) + (pltpu.roll(z, 2, 0) + pltpu.roll(z, 3, 0))
        back[k] = jnp.where(colour, through * error, z)
        behind = behind + contrib
    by_seg = exact_rows(jnp.concatenate(back, axis=1), o_ref[...])
    out = [by_seg[:, s * N : (s + 1) * N] for s in range(SEGS)] + [image]
    send_buf[3] = pad_rows(jnp.concatenate(out, axis=0)).T
    send(3)
    q_ref[...] = receive(3)

    def backward_a(s, _):
        def one(c, acc):
            at = place(s, c)
            q = pl.ds(pl.multiple_of(lax.rem(c, 4) * CHUNK, CHUNK), CHUNK)
            mine = q_ref[q, :]
            weight = w_ref[at, :]
            d_weight = jnp.zeros((CHUNK, SPAN), F32)
            new = []
            for ch in range(3):
                d = jnp.where(lane32 == 8 * s + 4 * (c // 4) + ch, mine, 0.0)
                d = jnp.sum(d, axis=1, keepdims=True)
                d_weight = d_weight + d * row(s, 6 + ch)
                g = weight * d
                g = (g[0:8] + g[8:16]) + (g[16:24] + g[24:32])
                new.append(acc[ch] + g)
            d_early = d_weight * weight
            w_ref[at, :] = d_early
            hi, lo = split2(d_early)
            hi_ref[at, :] = hi
            lo_ref[at, :] = lo
            return tuple(new)

        zero = jnp.zeros((8, SPAN), F32)
        acc = lax.fori_loop(0, CHUNKS, one, (zero, zero, zero))
        for ch in range(3):
            total = jnp.sum(acc[ch], axis=0, keepdims=True)
            if ch < 2:
                dp_ref[s, 6 + ch : 7 + ch, :] = total
            else:
                dpl_ref[s, 0:1, :] = total
        return 0

    lax.fori_loop(0, SEGS, backward_a, 0)

    later = onehot(iota((SPAN, SPAN), 0) > iota((SPAN, SPAN), 1))

    def back_sums(s, _):
        at = pl.ds(pl.multiple_of(s * PIX, PIX), PIX)
        x_ref[at, :] = mm(hi_ref[at, :], later) + mm(lo_ref[at, :], later)
        return 0

    lax.fori_loop(0, SEGS, back_sums, 0)

    def backward_b(s, _):
        def one(c, acc):
            at = place(s, c)
            q = pl.ds(pl.multiple_of(lax.rem(c, 4) * CHUNK, CHUNK), CHUNK)
            d = jnp.where(lane32 == 8 * s + 4 * (c // 4) + 3, q_ref[q, :], 0.0)
            d = jnp.sum(d, axis=1, keepdims=True)
            g0 = w_ref[at, :] - (x_ref[at, :] + d) * a_ref[at, :]
            dy = lines(s, c)
            g1 = g0 * dy
            g2 = g1 * dy
            return tuple(o + (g[0:16] + g[16:32]) for o, g in zip(acc, (g0, g1, g2)))

        zero = jnp.zeros((16, SPAN), F32)
        m0, m1, m2 = lax.fori_loop(0, CHUNKS, one, (zero, zero, zero))
        dx = delta_x(s)

        def down(x):
            return jnp.sum(x, axis=0, keepdims=True)

        s0, sx, sy = down(m0), down(m0 * dx), down(m1)
        sxx, sxy, syy = down(m0 * dx * dx), down(m1 * dx), down(m2)
        na, nb, nc = row(s, 2), row(s, 3), row(s, 4)
        dp_ref[s, 0:1, :] = -2.0 * na * sx - nb * sy
        dp_ref[s, 1:2, :] = -nb * sx - 2.0 * nc * sy
        dp_ref[s, 2:3, :] = 2.0 * na * sxx + nb * sxy
        dp_ref[s, 3:4, :] = 2.0 * nc * syy + nb * sxy
        dp_ref[s, 4:5, :] = -sxy * row(s, 9)
        dp_ref[s, 5:6, :] = s0 * row(s, 10)
        return 0

    lax.fori_loop(0, SEGS, backward_b, 0)

    main = jnp.concatenate([dp_ref[s] for s in range(SEGS)], axis=1)
    last = jnp.concatenate([dpl_ref[s, 0:1, :] for s in range(SEGS)], axis=1)
    send_buf[4] = pad_rows(spread(main, last, slot, e_ref[...])).T
    send(4)
    shown = q_ref[...].T
    for h in range(2):
        for ch in range(3):
            at = 32 + 4 * h + ch
            img_ref[ch, :, h * N : (h + 1) * N] = shown[at : at + 1]
    given = receive(4).T
    main = jnp.concatenate([given[8 * k : 8 * k + 8] for k in range(CAP)], axis=1)
    last = jnp.concatenate([given[64 + k : 65 + k] for k in range(CAP)], axis=1)
    grads = spread(main, last, high, ohj_ref[...])

    def adam(at, grad):
        moment = 0.9 * mom_ref[at] + 0.1 * grad
        second = 0.99 * sec_ref[at] + 0.01 * grad * grad
        nmom_ref[at] = moment
        nsec_ref[at] = second
        npar_ref[at] = par_ref[at] - 0.05 * moment / (jnp.sqrt(second) + 1e-08)

    for c in range(8):
        at = slice(c * N, (c + 1) * N)
        adam((slice(0, 8), at), grads[8 * c : 8 * c + 8])
        adam((slice(8, 9), at), grads[64 + c : 65 + c])

    for r in range(5):
        pltpu.make_async_remote_copy(
            src_ref=send_buf.at[r, pl.ds(0, N - 1)],
            dst_ref=recv_buf.at[r, pl.ds(0, N - 1)],
            send_sem=send_sem.at[r],
            recv_sem=recv_sem.at[r],
            device_id=(lax.rem(me + 1, N),),
            device_id_type=MESH,
        ).wait_send()


def nat_pad(x):
    return jnp.concatenate([x, jnp.zeros((16 - x.shape[0], x.shape[1]), BF16)], axis=0)


def per_device(params, moment, second, fetch_ids, seg_ids, seg_count, seg_perm, target):
    vmem = pl.BlockSpec(memory_space=pltpu.VMEM)
    smem = pl.BlockSpec(memory_space=pltpu.SMEM)
    shape = jax.ShapeDtypeStruct
    image, new_params, new_moment, new_second = pl.pallas_call(
        kernel,
        out_shape=(
            shape((3, 1, PIX), F32),
            shape(params.shape, F32),
            shape(params.shape, F32),
            shape(params.shape, F32),
        ),
        in_specs=[smem, smem] + [vmem] * 7,
        out_specs=(vmem,) * 4,
        scratch_shapes=[
            pltpu.VMEM((5, N, N), F32),
            pltpu.VMEM((5, N, N), F32),
            pltpu.VMEM((SEGS * SPAN, N), BF16),
            pltpu.VMEM((N, SEGS * SPAN), BF16),
            pltpu.VMEM((4 * N, SEGS * N), BF16),
            pltpu.VMEM((SEGS * N, 4 * N), BF16),
            pltpu.VMEM((CAP * N, N), BF16),
            pltpu.VMEM((SEGS, 16, SPAN), F32),
            pltpu.VMEM((N, N), F32),
            pltpu.VMEM((N, N), F32),
            pltpu.VMEM((SEGS * PIX, SPAN), F32),
            pltpu.VMEM((SEGS * PIX, SPAN), F32),
            pltpu.VMEM((SEGS * PIX, SPAN), BF16),
            pltpu.VMEM((SEGS * PIX, SPAN), BF16),
            pltpu.VMEM((SEGS * PIX, SPAN), F32),
            pltpu.VMEM((SEGS, 8, SPAN), F32),
            pltpu.VMEM((SEGS, 8, SPAN), F32),
            pltpu.SemaphoreType.DMA((5,)),
            pltpu.SemaphoreType.DMA((5,)),
        ],
        compiler_params=pltpu.CompilerParams(collective_id=0, has_side_effects=True),
        name="splat_step",
    )(
        seg_count,
        seg_perm,
        params,
        moment,
        second,
        fetch_ids[0].T,
        seg_ids,
        seg_perm.reshape(SEGS, N),
        jnp.transpose(target, (1, 0, 2)),
    )
    return (jnp.transpose(image, (1, 0, 2)), new_params, new_moment, new_second)


def solution(mesh):
    placed = (
        P(None, "dev"),
        P(None, "dev"),
        P(None, "dev"),
        P("dev", None, None),
        P("dev", None),
        P("dev"),
        P(),
        P("dev", None, None),
    )
    return jax.shard_map(
        per_device,
        mesh=mesh,
        in_specs=placed,
        out_specs=(P("dev", None, None), P(None, "dev"), P(None, "dev"), P(None, "dev")),
        check_vma=False,
    )
```

```python
import jax
import jax.numpy as jnp
from jax import lax
from jax.experimental import pallas as pl
from jax.experimental.pallas import tpu as pltpu
from jax.sharding import PartitionSpec as P

F32, BF16, I32 = jnp.float32, jnp.bfloat16, jnp.int32
MESH = pl.DeviceIdType.MESH
N = 128
SEGS = 4
SPAN = 256
PIX = 256
CHUNK = 32
CHUNKS = PIX // CHUNK
CAP = 8


def iota(shape, axis):
    return lax.broadcasted_iota(I32, shape, axis)


def onehot(cond):
    return jnp.where(cond, 1.0, 0.0).astype(BF16)


def mm(a, b):
    return jnp.dot(a, b, preferred_element_type=F32)


def split2(x):
    hi = x.astype(BF16)
    lo = (x - hi.astype(F32)).astype(BF16)
    return hi, lo


def split3(x):
    hi = x.astype(BF16)
    rest = x - hi.astype(F32)
    mid = rest.astype(BF16)
    lo = (rest - mid.astype(F32)).astype(BF16)
    return hi, mid, lo


def exact_rows(x, sel):
    n = x.shape[0]
    pad = -n % 16
    if pad:
        x = jnp.concatenate([x, jnp.zeros((pad, x.shape[1]), F32)], axis=0)
    out = mm(jnp.concatenate(split3(x), axis=0), sel)
    m = n + pad
    return (out[:n] + out[m : m + n]) + out[2 * m : 2 * m + n]


def pick(table, sel, high):
    got = exact_rows(table, sel)
    main = jnp.zeros((8, got.shape[1]), F32)
    for h in range(8):
        main = main + jnp.where(high == h, got[8 * h : 8 * h + 8], 0.0)
    last = jnp.where(iota((8, got.shape[1]), 0) == high, got[64:72], 0.0)
    return main, jnp.sum(last, axis=0, keepdims=True)


def spread(main, last, high, sel):
    rows = [jnp.where(high == h, main, 0.0) for h in range(8)]
    rows.append(jnp.where(iota(main.shape, 0) == high, last, 0.0))
    rows.append(jnp.zeros_like(main))
    x = jnp.concatenate(rows, axis=0)
    out = mm(jnp.concatenate(split2(x), axis=0), sel)
    return out[:72] + out[80:152]


def pad_rows(x):
    return jnp.concatenate([x, jnp.zeros((N - x.shape[0], x.shape[1]), F32)], axis=0)


def kernel(
    count_hbm, perm_hbm, par_hbm, fetch_hbm, ids_hbm, permv_hbm, tgt_hbm, img_ref, grad_ref, send_buf, recv_buf, e_ref, et_ref, o_ref, ot_ref, ohj_ref, rows_ref, f_ref, q_ref, a_ref, w_ref, hi_ref, lo_ref, x_ref, dp_ref, dpl_ref, count_ref, perm_ref, par_ref, fetch_ref, ids_ref, permv_ref, tgt_ref, send_sem, recv_sem, in_sem,
):
    me = lax.axis_index("dev")
    barrier = pltpu.get_barrier_semaphore()

    def greet(i, _):
        pl.semaphore_signal(
            barrier, inc=1, device_id=(lax.rem(me + i, N),), device_id_type=MESH
        )
        return 0

    lax.fori_loop(1, N, greet, 0)
    pairs = (
        (fetch_hbm, fetch_ref), (ids_hbm, ids_ref), (par_hbm, par_ref), (permv_hbm, permv_ref),
        (perm_hbm, perm_ref), (count_hbm, count_ref), (tgt_hbm, tgt_ref),
    )
    for n, (src, dst) in enumerate(pairs):
        pltpu.make_async_copy(src, dst, in_sem.at[n]).start()
    for n, (src, dst) in enumerate(pairs):
        pltpu.make_async_copy(src, dst, in_sem.at[n]).wait()

    X, Y = me // 32, lax.rem(me // 8, 4)
    Z, C = lax.rem(me // 2, 4), lax.rem(me, 2)
    near = [
        lax.rem(Z + dz, 4) * 2 + lax.rem(C + dc, 2)
        for dz in (2, 1, 3, 0)
        for dc in (0, 1)
    ]

    def push(r, to):
        pltpu.make_async_remote_copy(
            src_ref=send_buf.at[r, pl.ds(to, 1)],
            dst_ref=recv_buf.at[r, pl.ds(me, 1)],
            send_sem=send_sem.at[r],
            recv_sem=recv_sem.at[r],
            device_id=(to,),
            device_id_type=MESH,
        ).start()

    def ring(j):
        return lax.rem(2 + j * (j + 1) // 2, 4)

    def send(r):
        def column(i, _):
            base = lax.rem(X + ring(i // 4), 4) * 32 + lax.rem(Y + ring(lax.rem(i, 4)), 4) * 8
            for at in near:
                push(r, base + at)
            return 0

        lax.fori_loop(0, 15, column, 0, unroll=True)
        for at in near[:6] + near[7:]:
            push(r, X * 32 + Y * 8 + at)
        pltpu.make_async_copy(
            send_buf.at[r, pl.ds(me, 1)], recv_buf.at[r, pl.ds(me, 1)], recv_sem.at[r]
        ).start()

    def receive(r):
        pltpu.make_async_copy(send_buf.at[r], recv_buf.at[r], recv_sem.at[r]).wait()
        return recv_buf[r]

    ids = [ids_ref[s : s + 1, :] for s in range(SEGS)]
    for s in range(SEGS):
        for h in range(2):
            row = jnp.broadcast_to(ids[s][:, h * N : (h + 1) * N] // CAP, (N, N))
            at = (2 * s + h) * N
            sel = jnp.where(iota((N, N), 0) == row, 1.0, 0.0)
            et_ref[:, at : at + N] = sel.astype(BF16)
            e_ref[at : at + N, :] = sel.T.astype(BF16)
    slot = jnp.concatenate(ids, axis=1) % CAP
    table = [par_ref[0:8, c * N : (c + 1) * N] for c in range(8)]
    table += [par_ref[8:9, c * N : (c + 1) * N] for c in range(8)]
    table = jnp.concatenate(table, axis=0)

    send_buf[0] = pad_rows(fetch_ref[...].astype(F32)).T
    pl.semaphore_wait(barrier, N - 1)
    send(0)

    nat = permv_ref[...]
    nat = jnp.concatenate([nat // SEGS, nat % SEGS], axis=0).astype(F32).astype(BF16)
    col = iota((N, SEGS * N), 1)
    deal = mm(nat_pad(nat), onehot(iota((N, SEGS * N), 0) == 4 * (col % 32) + col // N))
    quarter = (iota((1, SEGS * N), 1) % N) // 32
    code = jnp.zeros((1, SEGS * N), F32)
    for a in range(4):
        code = code + jnp.where(
            quarter == a, deal[a : a + 1] + N * deal[4 + a : 5 + a], 0.0
        )
    for b in range(4):
        piece = jnp.broadcast_to(code[:, b * N : (b + 1) * N].astype(I32), (N, N))
        for k in range(4):
            sel = jnp.where(iota((N, N), 0) + k * N == piece, 1.0, 0.0)
            o_ref[k * N : (k + 1) * N, b * N : (b + 1) * N] = sel.astype(BF16)
            ot_ref[b * N : (b + 1) * N, k * N : (k + 1) * N] = sel.T.astype(BF16)
    tgt = []
    for h in range(2):
        tgt += [tgt_ref[ch, :, h * N : (h + 1) * N] for ch in range(3)]
        tgt.append(jnp.zeros((1, N), F32))
    tgt = jnp.concatenate([jnp.zeros((32, N), F32)] + tgt, axis=0)
    f_ref[...] = pad_rows(tgt).T

    got = receive(0).astype(I32)
    wanted = got.astype(F32).T[0:8].astype(I32)
    wanted = jnp.concatenate([wanted[k : k + 1] for k in range(CAP)], axis=1)
    high = wanted // N
    low = wanted % N
    oht = onehot(iota((N, CAP * N), 0) == low)
    main, last = pick(table, oht, high)
    out = [main[:, k * N : (k + 1) * N] for k in range(CAP)]
    out += [last[:, k * N : (k + 1) * N] for k in range(CAP)]
    send_buf[1] = pad_rows(jnp.concatenate(out, axis=0)).T
    send(1)

    lane = iota((N, N), 1)
    for k in range(CAP):
        ohj_ref[k * N : (k + 1) * N, :] = onehot(got[:, k : k + 1] % N == lane)
    arrived = receive(1).T
    main, last = pick(arrived[0:72], et_ref[...], slot)
    scale = jnp.exp(main)
    bend = jnp.tanh(main)
    gate = jax.nn.sigmoid(main)
    sa, sc = scale[2:3], scale[3:4]
    th, sg = bend[4:5], gate[5:6]
    cross = 0.8 * th * sa * sc
    step = iota((1, SPAN), 1)
    live = jnp.concatenate(
        [jnp.where(step < count_ref[s], 1.0, 0.0) for s in range(SEGS)], axis=1
    )
    rows = [
        main[0:1], main[1:2], -0.5 * (sa * sa), -cross, -0.5 * (sc * sc), 0.95 * sg * live,
        main[6:7], main[7:8], last, 0.8 * (1.0 - th * th) * sa * sc, 1.0 - sg,
    ]
    for s in range(SEGS):
        for i, row in enumerate(rows):
            rows_ref[s, i : i + 1, :] = row[:, s * SPAN : (s + 1) * SPAN]

    def tile_of(s):
        tile = perm_ref[me * SEGS + s] // SEGS
        return (tile % 8).astype(F32), (tile // 8).astype(F32)

    def row(s, i):
        return rows_ref[s, i : i + 1, :]

    fine_x = (iota((16, SPAN), 0).astype(F32) + 0.5) / 16.0

    def delta_x(s):
        return (tile_of(s)[0] + fine_x) - row(s, 0)

    def delta_y(s, line):
        at = tile_of(s)[1] + (line.astype(F32) + 0.5) / 16.0
        return at - row(s, 1)

    def twice(x):
        return jnp.concatenate([x, x], axis=0)

    def lines(s, c):
        return jnp.concatenate(
            [jnp.broadcast_to(delta_y(s, 2 * c + i), (16, SPAN)) for i in range(2)], axis=0
        )

    def place(s, c):
        return pl.ds(pl.multiple_of(s * PIX + c * CHUNK, CHUNK), CHUNK)

    lane32 = iota((CHUNK, N), 1)

    def forward_a(s, _):
        dx = delta_x(s)
        t1 = twice(row(s, 2) * dx * dx)
        t2 = twice(row(s, 3) * dx)

        def one(c, _):
            dy = lines(s, c)
            alpha = row(s, 5) * jnp.exp(t1 + dy * (t2 + row(s, 4) * dy))
            logt = jnp.log(1.0 - alpha)
            at = place(s, c)
            a_ref[at, :] = alpha
            hi, lo = split2(logt)
            hi_ref[at, :] = hi
            lo_ref[at, :] = lo
            total = jnp.sum(logt, axis=1, keepdims=True)
            q = pl.ds(pl.multiple_of(lax.rem(c, 4) * CHUNK, CHUNK), CHUNK)
            f_ref[q, :] = jnp.where(
                lane32 == 8 * s + 4 * (c // 4) + 3, total, f_ref[q, :]
            )
            return 0

        return lax.fori_loop(0, CHUNKS, one, 0, unroll=True)

    lax.fori_loop(0, SEGS, forward_a, 0, unroll=True)

    tri = iota((SPAN, SPAN), 0) < iota((SPAN, SPAN), 1)
    earlier = onehot(tri)

    def sums(s, _):
        at = pl.ds(pl.multiple_of(s * PIX, PIX), PIX)
        x_ref[at, :] = mm(hi_ref[at, :], earlier) + mm(lo_ref[at, :], earlier)
        return 0

    lax.fori_loop(0, SEGS, sums, 0, unroll=True)

    def forward_b(s, _):
        def one(c, _):
            at = place(s, c)
            alpha = a_ref[at, :]
            weight = jnp.exp(x_ref[at, :]) * alpha
            w_ref[at, :] = weight
            a_ref[at, :] = alpha / (1.0 - alpha)
            q = pl.ds(pl.multiple_of(lax.rem(c, 4) * CHUNK, CHUNK), CHUNK)
            kept = f_ref[q, :]
            for ch in range(3):
                total = jnp.sum(weight * row(s, 6 + ch), axis=1, keepdims=True)
                kept = jnp.where(lane32 == 8 * s + 4 * (c // 4) + ch, total, kept)
            f_ref[q, :] = kept
            return 0

        return lax.fori_loop(0, CHUNKS, one, 0, unroll=True)

    lax.fori_loop(0, SEGS, forward_b, 0, unroll=True)

    send_buf[2] = f_ref[...]
    send(2)
    seen = receive(2).T
    by_seg = jnp.concatenate([seen[8 * s : 8 * s + 8] for s in range(SEGS)], axis=1)
    target = seen[32:40]
    by_tile = exact_rows(by_seg, ot_ref[...])
    sub = iota((8, N), 0) % 4
    colour = sub < 3
    before = jnp.zeros((8, N), F32)
    image = jnp.zeros((8, N), F32)
    terms = []
    for k in range(4):
        part = by_tile[:, k * N : (k + 1) * N]
        through = jnp.exp(before)
        contrib = jnp.where(colour, through * part, 0.0)
        terms.append((through, contrib))
        image = image + contrib
        log = jnp.where(colour, 0.0, part)
        log = log + pltpu.roll(log, 7, 0)
        before = before + (log + pltpu.roll(log, 6, 0))
    error = jnp.where(colour, image - target, 0.0)
    behind = jnp.zeros((8, N), F32)
    back = [None] * 4
    for k in (3, 2, 1, 0):
        through, contrib = terms[k]
        z = error * behind
        z = pltpu.roll(z, 1, 0) + (pltpu.roll(z, 2, 0) + pltpu.roll(z, 3, 0))
        back[k] = jnp.where(colour, through * error, z)
        behind = behind + contrib
    by_seg = exact_rows(jnp.concatenate(back, axis=1), o_ref[...])
    out = [by_seg[:, s * N : (s + 1) * N] for s in range(SEGS)] + [image]
    send_buf[3] = pad_rows(jnp.concatenate(out, axis=0)).T
    send(3)
    q_ref[...] = receive(3)

    def backward_a(s, _):
        def one(c, acc):
            at = place(s, c)
            q = pl.ds(pl.multiple_of(lax.rem(c, 4) * CHUNK, CHUNK), CHUNK)
            mine = q_ref[q, :]
            weight = w_ref[at, :]
            d_weight = jnp.zeros((CHUNK, SPAN), F32)
            new = []
            for ch in range(3):
                d = jnp.where(lane32 == 8 * s + 4 * (c // 4) + ch, mine, 0.0)
                d = jnp.sum(d, axis=1, keepdims=True)
                d_weight = d_weight + d * row(s, 6 + ch)
                g = weight * d
                g = (g[0:8] + g[8:16]) + (g[16:24] + g[24:32])
                new.append(acc[ch] + g)
            d_early = d_weight * weight
            w_ref[at, :] = d_early
            hi, lo = split2(d_early)
            hi_ref[at, :] = hi
            lo_ref[at, :] = lo
            return tuple(new)

        zero = jnp.zeros((8, SPAN), F32)
        acc = lax.fori_loop(0, CHUNKS, one, (zero, zero, zero), unroll=True)
        for ch in range(3):
            total = jnp.sum(acc[ch], axis=0, keepdims=True)
            if ch < 2:
                dp_ref[s, 6 + ch : 7 + ch, :] = total
            else:
                dpl_ref[s, 0:1, :] = total
        return 0

    lax.fori_loop(0, SEGS, backward_a, 0, unroll=True)

    later = onehot(iota((SPAN, SPAN), 0) > iota((SPAN, SPAN), 1))

    def back_sums(s, _):
        at = pl.ds(pl.multiple_of(s * PIX, PIX), PIX)
        x_ref[at, :] = mm(hi_ref[at, :], later) + mm(lo_ref[at, :], later)
        return 0

    lax.fori_loop(0, SEGS, back_sums, 0, unroll=True)

    def backward_b(s, _):
        def one(c, acc):
            at = place(s, c)
            q = pl.ds(pl.multiple_of(lax.rem(c, 4) * CHUNK, CHUNK), CHUNK)
            d = jnp.where(lane32 == 8 * s + 4 * (c // 4) + 3, q_ref[q, :], 0.0)
            d = jnp.sum(d, axis=1, keepdims=True)
            g0 = w_ref[at, :] - (x_ref[at, :] + d) * a_ref[at, :]
            dy = lines(s, c)
            g1 = g0 * dy
            g2 = g1 * dy
            return tuple(o + (g[0:16] + g[16:32]) for o, g in zip(acc, (g0, g1, g2)))

        zero = jnp.zeros((16, SPAN), F32)
        m0, m1, m2 = lax.fori_loop(0, CHUNKS, one, (zero, zero, zero), unroll=True)
        dx = delta_x(s)

        def down(x):
            return jnp.sum(x, axis=0, keepdims=True)

        s0, sx, sy = down(m0), down(m0 * dx), down(m1)
        sxx, sxy, syy = down(m0 * dx * dx), down(m1 * dx), down(m2)
        na, nb, nc = row(s, 2), row(s, 3), row(s, 4)
        dp_ref[s, 0:1, :] = -2.0 * na * sx - nb * sy
        dp_ref[s, 1:2, :] = -nb * sx - 2.0 * nc * sy
        dp_ref[s, 2:3, :] = 2.0 * na * sxx + nb * sxy
        dp_ref[s, 3:4, :] = 2.0 * nc * syy + nb * sxy
        dp_ref[s, 4:5, :] = -sxy * row(s, 9)
        dp_ref[s, 5:6, :] = s0 * row(s, 10)
        return 0

    lax.fori_loop(0, SEGS, backward_b, 0, unroll=True)

    main = jnp.concatenate([dp_ref[s] for s in range(SEGS)], axis=1)
    last = jnp.concatenate([dpl_ref[s, 0:1, :] for s in range(SEGS)], axis=1)
    send_buf[4] = pad_rows(spread(main, last, slot, e_ref[...])).T
    send(4)
    shown = q_ref[...].T
    for h in range(2):
        for ch in range(3):
            at = 32 + 4 * h + ch
            img_ref[ch, :, h * N : (h + 1) * N] = shown[at : at + 1]
    given = receive(4).T
    main = jnp.concatenate([given[8 * k : 8 * k + 8] for k in range(CAP)], axis=1)
    last = jnp.concatenate([given[64 + k : 65 + k] for k in range(CAP)], axis=1)
    grads = spread(main, last, high, ohj_ref[...])

    grad_ref[...] = grads

    for r in range(5):
        pltpu.make_async_remote_copy(
            src_ref=send_buf.at[r, pl.ds(0, N - 1)],
            dst_ref=recv_buf.at[r, pl.ds(0, N - 1)],
            send_sem=send_sem.at[r],
            recv_sem=recv_sem.at[r],
            device_id=(lax.rem(me + 1, N),),
            device_id_type=MESH,
        ).wait_send()


def update(
    grad_ref, img_ref, par_ref, mom_ref, sec_ref, oimg_ref, npar_ref, nmom_ref, nsec_ref
):
    oimg_ref[...] = img_ref[...]

    def adam(at, grad):
        moment = 0.9 * mom_ref[at] + 0.1 * grad
        second = 0.99 * sec_ref[at] + 0.01 * grad * grad
        nmom_ref[at] = moment
        nsec_ref[at] = second
        npar_ref[at] = par_ref[at] - 0.05 * moment / (jnp.sqrt(second) + 1e-08)

    for c in range(8):
        at = slice(c * N, (c + 1) * N)
        adam((slice(0, 8), at), grad_ref[8 * c : 8 * c + 8])
        adam((slice(8, 9), at), grad_ref[64 + c : 65 + c])


def nat_pad(x):
    return jnp.concatenate([x, jnp.zeros((16 - x.shape[0], x.shape[1]), BF16)], axis=0)


def per_device(params, moment, second, fetch_ids, seg_ids, seg_count, seg_perm, target):
    vmem = pl.BlockSpec(memory_space=pltpu.VMEM)
    hbm = pl.BlockSpec(memory_space=pltpu.HBM)
    shape = jax.ShapeDtypeStruct
    image, grads = pl.pallas_call(
        kernel,
        out_shape=(shape((3, 1, PIX), F32), shape((72, N), F32)),
        in_specs=[hbm] * 7,
        out_specs=(vmem,) * 2,
        scratch_shapes=[
            pltpu.VMEM((5, N, N), F32),
            pltpu.VMEM((5, N, N), F32),
            pltpu.VMEM((SEGS * SPAN, N), BF16),
            pltpu.VMEM((N, SEGS * SPAN), BF16),
            pltpu.VMEM((4 * N, SEGS * N), BF16),
            pltpu.VMEM((SEGS * N, 4 * N), BF16),
            pltpu.VMEM((CAP * N, N), BF16),
            pltpu.VMEM((SEGS, 16, SPAN), F32),
            pltpu.VMEM((N, N), F32),
            pltpu.VMEM((N, N), F32),
            pltpu.VMEM((SEGS * PIX, SPAN), F32),
            pltpu.VMEM((SEGS * PIX, SPAN), F32),
            pltpu.VMEM((SEGS * PIX, SPAN), BF16),
            pltpu.VMEM((SEGS * PIX, SPAN), BF16),
            pltpu.VMEM((SEGS * PIX, SPAN), F32),
            pltpu.VMEM((SEGS, 8, SPAN), F32),
            pltpu.VMEM((SEGS, 8, SPAN), F32),
            pltpu.SMEM((SEGS,), I32),
            pltpu.SMEM((SEGS * N,), I32),
            pltpu.VMEM(params.shape, F32),
            pltpu.VMEM((CAP, N), I32),
            pltpu.VMEM((SEGS, SPAN), I32),
            pltpu.VMEM((SEGS, N), I32),
            pltpu.VMEM((3, 1, PIX), F32),
            pltpu.SemaphoreType.DMA((5,)),
            pltpu.SemaphoreType.DMA((5,)),
            pltpu.SemaphoreType.DMA((7,)),
        ],
        compiler_params=pltpu.CompilerParams(collective_id=0, has_side_effects=True),
        name="splat_step",
    )(
        seg_count,
        seg_perm,
        params,
        fetch_ids[0].T,
        seg_ids,
        seg_perm.reshape(SEGS, N),
        jnp.transpose(target, (1, 0, 2)),
    )
    image, new_params, new_moment, new_second = pl.pallas_call(
        update,
        out_shape=(shape((3, 1, PIX), F32),) + (shape(params.shape, F32),) * 3,
        in_specs=[vmem] * 5,
        out_specs=(vmem,) * 4,
        name="adam",
    )(grads, image, params, moment, second)
    return (jnp.transpose(image, (1, 0, 2)), new_params, new_moment, new_second)


def solution(mesh):
    placed = (
        P(None, "dev"),
        P(None, "dev"),
        P(None, "dev"),
        P("dev", None, None),
        P("dev", None),
        P("dev"),
        P(),
        P("dev", None, None),
    )
    return jax.shard_map(
        per_device,
        mesh=mesh,
        in_specs=placed,
        out_specs=(P("dev", None, None), P(None, "dev"), P(None, "dev"), P(None, "dev")),
        check_vma=False,
    )
```

```python
import jax
import jax.numpy as jnp
from jax import lax
from jax.experimental import pallas as pl
from jax.experimental.pallas import tpu as pltpu
from jax.sharding import PartitionSpec as P

F32, BF16, I32 = jnp.float32, jnp.bfloat16, jnp.int32
MESH = pl.DeviceIdType.MESH
N = 128
SEGS = 4
SPAN = 256
PIX = 256
CHUNK = 32
CHUNKS = PIX // CHUNK
CAP = 8
FAR_FIRST = sorted(
    (-min(a, 4 - a) - min(b, 4 - b) - min(c // 2, 4 - c // 2), a, b, c)
    for a in range(4)
    for b in range(4)
    for c in range(8)
    if a or b or c
)


def iota(shape, axis):
    return lax.broadcasted_iota(I32, shape, axis)


def onehot(cond):
    return jnp.where(cond, 1.0, 0.0).astype(BF16)


def mm(a, b):
    return jnp.dot(a, b, preferred_element_type=F32)


def split2(x):
    hi = x.astype(BF16)
    lo = (x - hi.astype(F32)).astype(BF16)
    return hi, lo


def split3(x):
    hi = x.astype(BF16)
    rest = x - hi.astype(F32)
    mid = rest.astype(BF16)
    lo = (rest - mid.astype(F32)).astype(BF16)
    return hi, mid, lo


def exact_rows(x, sel):
    n = x.shape[0]
    pad = -n % 16
    if pad:
        x = jnp.concatenate([x, jnp.zeros((pad, x.shape[1]), F32)], axis=0)
    out = mm(jnp.concatenate(split3(x), axis=0), sel)
    m = n + pad
    return (out[:n] + out[m : m + n]) + out[2 * m : 2 * m + n]


def pick(table, sel, high):
    got = exact_rows(table, sel)
    main = jnp.zeros((8, got.shape[1]), F32)
    for h in range(8):
        main = main + jnp.where(high == h, got[8 * h : 8 * h + 8], 0.0)
    last = jnp.where(iota((8, got.shape[1]), 0) == high, got[64:72], 0.0)
    return main, jnp.sum(last, axis=0, keepdims=True)


def spread(main, last, high, sel):
    rows = [jnp.where(high == h, main, 0.0) for h in range(8)]
    rows.append(jnp.where(iota(main.shape, 0) == high, last, 0.0))
    rows.append(jnp.zeros_like(main))
    x = jnp.concatenate(rows, axis=0)
    out = mm(jnp.concatenate(split2(x), axis=0), sel)
    return out[:72] + out[80:152]


def pad_rows(x):
    return jnp.concatenate([x, jnp.zeros((N - x.shape[0], x.shape[1]), F32)], axis=0)


def kernel(
    count_hbm, perm_hbm, par_hbm, fetch_hbm, ids_hbm, permv_hbm, tgt_hbm, mom_hbm, sec_hbm, img_ref, npar_ref, nmom_ref, nsec_ref, send_buf, recv_buf, e_ref, et_ref, o_ref, ot_ref, ohj_ref, rows_ref, f_ref, q_ref, a_ref, w_ref, hi_ref, lo_ref, x_ref, dp_ref, dpl_ref, count_ref, perm_ref, par_ref, fetch_ref, ids_ref, permv_ref, tgt_ref, mom_ref, sec_ref, send_sem, recv_sem, in_sem,
):
    me = lax.axis_index("dev")
    barrier = pltpu.get_barrier_semaphore()

    X, Y = me // 32, lax.rem(me // 8, 4)
    Z, C = lax.rem(me // 2, 4), lax.rem(me, 2)
    planes = [[lax.rem(X + d, 4) * 32 for d in range(4)], [lax.rem(Y + d, 4) * 8 for d in range(4)]]
    near = [lax.rem(Z + d // 2, 4) * 2 + lax.rem(C + d, 2) for d in range(8)]
    others = [planes[0][a] + planes[1][b] + near[c] for _, a, b, c in FAR_FIRST]
    for to in others:
        pl.semaphore_signal(barrier, inc=1, device_id=(to,), device_id_type=MESH)
    pairs = (
        (fetch_hbm, fetch_ref), (ids_hbm, ids_ref), (par_hbm, par_ref), (permv_hbm, permv_ref),
        (perm_hbm, perm_ref), (count_hbm, count_ref), (tgt_hbm, tgt_ref), (mom_hbm, mom_ref),
        (sec_hbm, sec_ref),
    )
    for n, (src, dst) in enumerate(pairs):
        pltpu.make_async_copy(src, dst, in_sem.at[n]).start()
    for n, (src, dst) in enumerate(pairs):
        pltpu.make_async_copy(src, dst, in_sem.at[n]).wait()

    def push(r, to):
        pltpu.make_async_remote_copy(
            src_ref=send_buf.at[r, pl.ds(to, 1)],
            dst_ref=recv_buf.at[r, pl.ds(me, 1)],
            send_sem=send_sem.at[r],
            recv_sem=recv_sem.at[r],
            device_id=(to,),
            device_id_type=MESH,
        ).start()

    def send(r):
        for to in others:
            push(r, to)
        pltpu.make_async_copy(
            send_buf.at[r, pl.ds(me, 1)], recv_buf.at[r, pl.ds(me, 1)], recv_sem.at[r]
        ).start()

    def receive(r):
        pltpu.make_async_copy(send_buf.at[r], recv_buf.at[r], recv_sem.at[r]).wait()
        return recv_buf[r]

    ids = [ids_ref[s : s + 1, :] for s in range(SEGS)]
    for s in range(SEGS):
        for h in range(2):
            row = jnp.broadcast_to(ids[s][:, h * N : (h + 1) * N] // CAP, (N, N))
            at = (2 * s + h) * N
            sel = jnp.where(iota((N, N), 0) == row, 1.0, 0.0)
            et_ref[:, at : at + N] = sel.astype(BF16)
            e_ref[at : at + N, :] = sel.T.astype(BF16)
    slot = jnp.concatenate(ids, axis=1) % CAP
    table = [par_ref[0:8, c * N : (c + 1) * N] for c in range(8)]
    table += [par_ref[8:9, c * N : (c + 1) * N] for c in range(8)]
    table = jnp.concatenate(table, axis=0)

    send_buf[0] = pad_rows(fetch_ref[...].astype(F32)).T
    pl.semaphore_wait(barrier, N - 1)
    send(0)

    nat = permv_ref[...]
    nat = jnp.concatenate([nat // SEGS, nat % SEGS], axis=0).astype(F32).astype(BF16)
    col = iota((N, SEGS * N), 1)
    deal = mm(nat_pad(nat), onehot(iota((N, SEGS * N), 0) == 4 * (col % 32) + col // N))
    quarter = (iota((1, SEGS * N), 1) % N) // 32
    code = jnp.zeros((1, SEGS * N), F32)
    for a in range(4):
        code = code + jnp.where(
            quarter == a, deal[a : a + 1] + N * deal[4 + a : 5 + a], 0.0
        )
    for b in range(4):
        piece = jnp.broadcast_to(code[:, b * N : (b + 1) * N].astype(I32), (N, N))
        for k in range(4):
            sel = jnp.where(iota((N, N), 0) + k * N == piece, 1.0, 0.0)
            o_ref[k * N : (k + 1) * N, b * N : (b + 1) * N] = sel.astype(BF16)
            ot_ref[b * N : (b + 1) * N, k * N : (k + 1) * N] = sel.T.astype(BF16)
    tgt = []
    for h in range(2):
        tgt += [tgt_ref[ch, :, h * N : (h + 1) * N] for ch in range(3)]
        tgt.append(jnp.zeros((1, N), F32))
    tgt = jnp.concatenate([jnp.zeros((32, N), F32)] + tgt, axis=0)
    f_ref[...] = pad_rows(tgt).T

    got = receive(0).astype(I32)
    wanted = got.astype(F32).T[0:8].astype(I32)
    wanted = jnp.concatenate([wanted[k : k + 1] for k in range(CAP)], axis=1)
    high = wanted // N
    low = wanted % N
    oht = onehot(iota((N, CAP * N), 0) == low)
    main, last = pick(table, oht, high)
    out = [main[:, k * N : (k + 1) * N] for k in range(CAP)]
    out += [last[:, k * N : (k + 1) * N] for k in range(CAP)]
    send_buf[1] = pad_rows(jnp.concatenate(out, axis=0)).T
    send(1)

    lane = iota((N, N), 1)
    for k in range(CAP):
        ohj_ref[k * N : (k + 1) * N, :] = onehot(got[:, k : k + 1] % N == lane)
    arrived = receive(1).T
    main, last = pick(arrived[0:72], et_ref[...], slot)
    scale = jnp.exp(main)
    bend = jnp.tanh(main)
    gate = jax.nn.sigmoid(main)
    sa, sc = scale[2:3], scale[3:4]
    th, sg = bend[4:5], gate[5:6]
    cross = 0.8 * th * sa * sc
    step = iota((1, SPAN), 1)
    live = jnp.concatenate(
        [jnp.where(step < count_ref[s], 1.0, 0.0) for s in range(SEGS)], axis=1
    )
    rows = [
        main[0:1], main[1:2], -0.5 * (sa * sa), -cross, -0.5 * (sc * sc), 0.95 * sg * live,
        main[6:7], main[7:8], last, 0.8 * (1.0 - th * th) * sa * sc, 1.0 - sg,
    ]
    for s in range(SEGS):
        for i, row in enumerate(rows):
            rows_ref[s, i : i + 1, :] = row[:, s * SPAN : (s + 1) * SPAN]

    def tile_of(s):
        tile = perm_ref[me * SEGS + s] // SEGS
        return (tile % 8).astype(F32), (tile // 8).astype(F32)

    def row(s, i):
        return rows_ref[s, i : i + 1, :]

    fine_x = (iota((16, SPAN), 0).astype(F32) + 0.5) / 16.0

    def delta_x(s):
        return (tile_of(s)[0] + fine_x) - row(s, 0)

    def delta_y(s, line):
        at = tile_of(s)[1] + (line.astype(F32) + 0.5) / 16.0
        return at - row(s, 1)

    def twice(x):
        return jnp.concatenate([x, x], axis=0)

    def lines(s, c):
        return jnp.concatenate(
            [jnp.broadcast_to(delta_y(s, 2 * c + i), (16, SPAN)) for i in range(2)], axis=0
        )

    def place(s, c):
        return pl.ds(pl.multiple_of(s * PIX + c * CHUNK, CHUNK), CHUNK)

    lane32 = iota((CHUNK, N), 1)

    def forward_a(s, _):
        dx = delta_x(s)
        t1 = twice(row(s, 2) * dx * dx)
        t2 = twice(row(s, 3) * dx)

        def one(c, _):
            dy = lines(s, c)
            alpha = row(s, 5) * jnp.exp(t1 + dy * (t2 + row(s, 4) * dy))
            logt = jnp.log(1.0 - alpha)
            at = place(s, c)
            a_ref[at, :] = alpha
            hi, lo = split2(logt)
            hi_ref[at, :] = hi
            lo_ref[at, :] = lo
            total = jnp.sum(logt, axis=1, keepdims=True)
            q = pl.ds(pl.multiple_of(lax.rem(c, 4) * CHUNK, CHUNK), CHUNK)
            f_ref[q, :] = jnp.where(
                lane32 == 8 * s + 4 * (c // 4) + 3, total, f_ref[q, :]
            )
            return 0

        return lax.fori_loop(0, CHUNKS, one, 0, unroll=True)

    lax.fori_loop(0, SEGS, forward_a, 0, unroll=True)

    tri = iota((SPAN, SPAN), 0) < iota((SPAN, SPAN), 1)
    earlier = onehot(tri)

    def sums(s, _):
        at = pl.ds(pl.multiple_of(s * PIX, PIX), PIX)
        x_ref[at, :] = mm(hi_ref[at, :], earlier) + mm(lo_ref[at, :], earlier)
        return 0

    lax.fori_loop(0, SEGS, sums, 0, unroll=True)

    def forward_b(s, _):
        def one(c, _):
            at = place(s, c)
            alpha = a_ref[at, :]
            weight = jnp.exp(x_ref[at, :]) * alpha
            w_ref[at, :] = weight
            a_ref[at, :] = alpha / (1.0 - alpha)
            q = pl.ds(pl.multiple_of(lax.rem(c, 4) * CHUNK, CHUNK), CHUNK)
            kept = f_ref[q, :]
            for ch in range(3):
                total = jnp.sum(weight * row(s, 6 + ch), axis=1, keepdims=True)
                kept = jnp.where(lane32 == 8 * s + 4 * (c // 4) + ch, total, kept)
            f_ref[q, :] = kept
            return 0

        return lax.fori_loop(0, CHUNKS, one, 0, unroll=True)

    lax.fori_loop(0, SEGS, forward_b, 0, unroll=True)

    send_buf[2] = f_ref[...]
    send(2)
    seen = receive(2).T
    by_seg = jnp.concatenate([seen[8 * s : 8 * s + 8] for s in range(SEGS)], axis=1)
    target = seen[32:40]
    by_tile = exact_rows(by_seg, ot_ref[...])
    sub = iota((8, N), 0) % 4
    colour = sub < 3
    before = jnp.zeros((8, N), F32)
    image = jnp.zeros((8, N), F32)
    terms = []
    for k in range(4):
        part = by_tile[:, k * N : (k + 1) * N]
        through = jnp.exp(before)
        contrib = jnp.where(colour, through * part, 0.0)
        terms.append((through, contrib))
        image = image + contrib
        log = jnp.where(colour, 0.0, part)
        log = log + pltpu.roll(log, 7, 0)
        before = before + (log + pltpu.roll(log, 6, 0))
    error = jnp.where(colour, image - target, 0.0)
    behind = jnp.zeros((8, N), F32)
    back = [None] * 4
    for k in (3, 2, 1, 0):
        through, contrib = terms[k]
        z = error * behind
        z = pltpu.roll(z, 1, 0) + (pltpu.roll(z, 2, 0) + pltpu.roll(z, 3, 0))
        back[k] = jnp.where(colour, through * error, z)
        behind = behind + contrib
    by_seg = exact_rows(jnp.concatenate(back, axis=1), o_ref[...])
    out = [by_seg[:, s * N : (s + 1) * N] for s in range(SEGS)] + [image]
    send_buf[3] = pad_rows(jnp.concatenate(out, axis=0)).T
    send(3)
    q_ref[...] = receive(3)

    def backward_a(s, _):
        def one(c, acc):
            at = place(s, c)
            q = pl.ds(pl.multiple_of(lax.rem(c, 4) * CHUNK, CHUNK), CHUNK)
            mine = q_ref[q, :]
            weight = w_ref[at, :]
            d_weight = jnp.zeros((CHUNK, SPAN), F32)
            new = []
            for ch in range(3):
                d = jnp.where(lane32 == 8 * s + 4 * (c // 4) + ch, mine, 0.0)
                d = jnp.sum(d, axis=1, keepdims=True)
                d_weight = d_weight + d * row(s, 6 + ch)
                g = weight * d
                g = (g[0:8] + g[8:16]) + (g[16:24] + g[24:32])
                new.append(acc[ch] + g)
            d_early = d_weight * weight
            w_ref[at, :] = d_early
            hi, lo = split2(d_early)
            hi_ref[at, :] = hi
            lo_ref[at, :] = lo
            return tuple(new)

        zero = jnp.zeros((8, SPAN), F32)
        acc = lax.fori_loop(0, CHUNKS, one, (zero, zero, zero), unroll=True)
        for ch in range(3):
            total = jnp.sum(acc[ch], axis=0, keepdims=True)
            if ch < 2:
                dp_ref[s, 6 + ch : 7 + ch, :] = total
            else:
                dpl_ref[s, 0:1, :] = total
        return 0

    lax.fori_loop(0, SEGS, backward_a, 0, unroll=True)

    later = onehot(iota((SPAN, SPAN), 0) > iota((SPAN, SPAN), 1))

    def back_sums(s, _):
        at = pl.ds(pl.multiple_of(s * PIX, PIX), PIX)
        x_ref[at, :] = mm(hi_ref[at, :], later) + mm(lo_ref[at, :], later)
        return 0

    lax.fori_loop(0, SEGS, back_sums, 0, unroll=True)

    def backward_b(s, _):
        def one(c, acc):
            at = place(s, c)
            q = pl.ds(pl.multiple_of(lax.rem(c, 4) * CHUNK, CHUNK), CHUNK)
            d = jnp.where(lane32 == 8 * s + 4 * (c // 4) + 3, q_ref[q, :], 0.0)
            d = jnp.sum(d, axis=1, keepdims=True)
            g0 = w_ref[at, :] - (x_ref[at, :] + d) * a_ref[at, :]
            dy = lines(s, c)
            g1 = g0 * dy
            g2 = g1 * dy
            return tuple(o + (g[0:16] + g[16:32]) for o, g in zip(acc, (g0, g1, g2)))

        zero = jnp.zeros((16, SPAN), F32)
        m0, m1, m2 = lax.fori_loop(0, CHUNKS, one, (zero, zero, zero), unroll=True)
        dx = delta_x(s)

        def down(x):
            return jnp.sum(x, axis=0, keepdims=True)

        s0, sx, sy = down(m0), down(m0 * dx), down(m1)
        sxx, sxy, syy = down(m0 * dx * dx), down(m1 * dx), down(m2)
        na, nb, nc = row(s, 2), row(s, 3), row(s, 4)
        dp_ref[s, 0:1, :] = -2.0 * na * sx - nb * sy
        dp_ref[s, 1:2, :] = -nb * sx - 2.0 * nc * sy
        dp_ref[s, 2:3, :] = 2.0 * na * sxx + nb * sxy
        dp_ref[s, 3:4, :] = 2.0 * nc * syy + nb * sxy
        dp_ref[s, 4:5, :] = -sxy * row(s, 9)
        dp_ref[s, 5:6, :] = s0 * row(s, 10)
        return 0

    lax.fori_loop(0, SEGS, backward_b, 0, unroll=True)

    main = jnp.concatenate([dp_ref[s] for s in range(SEGS)], axis=1)
    last = jnp.concatenate([dpl_ref[s, 0:1, :] for s in range(SEGS)], axis=1)
    send_buf[4] = pad_rows(spread(main, last, slot, e_ref[...])).T
    send(4)
    shown = q_ref[...].T
    for h in range(2):
        for ch in range(3):
            at = 32 + 4 * h + ch
            img_ref[ch, :, h * N : (h + 1) * N] = shown[at : at + 1]
    given = receive(4).T
    main = jnp.concatenate([given[8 * k : 8 * k + 8] for k in range(CAP)], axis=1)
    last = jnp.concatenate([given[64 + k : 65 + k] for k in range(CAP)], axis=1)
    grads = spread(main, last, high, ohj_ref[...])


    def adam(at, grad):
        moment = 0.9 * mom_ref[at] + 0.1 * grad
        second = 0.99 * sec_ref[at] + 0.01 * grad * grad
        nmom_ref[at] = moment
        nsec_ref[at] = second
        npar_ref[at] = par_ref[at] - 0.05 * moment / (jnp.sqrt(second) + 1e-08)

    for c in range(8):
        at = slice(c * N, (c + 1) * N)
        adam((slice(0, 8), at), grads[8 * c : 8 * c + 8])
        adam((slice(8, 9), at), grads[64 + c : 65 + c])

    for r in range(5):
        pltpu.make_async_remote_copy(
            src_ref=send_buf.at[r, pl.ds(0, N - 1)],
            dst_ref=recv_buf.at[r, pl.ds(0, N - 1)],
            send_sem=send_sem.at[r],
            recv_sem=recv_sem.at[r],
            device_id=(lax.rem(me + 1, N),),
            device_id_type=MESH,
        ).wait_send()


def store(*refs):
    sems = refs[8]
    copies = [pltpu.make_async_copy(refs[i], refs[4 + i], sems.at[i]) for i in range(4)]
    for copy in copies:
        copy.start()
    for copy in copies:
        copy.wait()


def nat_pad(x):
    return jnp.concatenate([x, jnp.zeros((16 - x.shape[0], x.shape[1]), BF16)], axis=0)


def per_device(params, moment, second, fetch_ids, seg_ids, seg_count, seg_perm, target):
    vmem = pl.BlockSpec(memory_space=pltpu.VMEM)
    hbm = pl.BlockSpec(memory_space=pltpu.HBM)
    shape = jax.ShapeDtypeStruct
    results = pl.pallas_call(
        kernel,
        out_shape=(shape((3, 1, PIX), F32),) + (shape(params.shape, F32),) * 3,
        in_specs=[hbm] * 9,
        out_specs=(vmem,) * 4,
        scratch_shapes=[
            pltpu.VMEM((5, N, N), F32),
            pltpu.VMEM((5, N, N), F32),
            pltpu.VMEM((SEGS * SPAN, N), BF16),
            pltpu.VMEM((N, SEGS * SPAN), BF16),
            pltpu.VMEM((4 * N, SEGS * N), BF16),
            pltpu.VMEM((SEGS * N, 4 * N), BF16),
            pltpu.VMEM((CAP * N, N), BF16),
            pltpu.VMEM((SEGS, 16, SPAN), F32),
            pltpu.VMEM((N, N), F32),
            pltpu.VMEM((N, N), F32),
            pltpu.VMEM((SEGS * PIX, SPAN), F32),
            pltpu.VMEM((SEGS * PIX, SPAN), F32),
            pltpu.VMEM((SEGS * PIX, SPAN), BF16),
            pltpu.VMEM((SEGS * PIX, SPAN), BF16),
            pltpu.VMEM((SEGS * PIX, SPAN), F32),
            pltpu.VMEM((SEGS, 8, SPAN), F32),
            pltpu.VMEM((SEGS, 8, SPAN), F32),
            pltpu.SMEM((SEGS,), I32),
            pltpu.SMEM((SEGS * N,), I32),
            pltpu.VMEM(params.shape, F32),
            pltpu.VMEM((CAP, N), I32),
            pltpu.VMEM((SEGS, SPAN), I32),
            pltpu.VMEM((SEGS, N), I32),
            pltpu.VMEM((3, 1, PIX), F32),
            pltpu.VMEM(params.shape, F32),
            pltpu.VMEM(params.shape, F32),
            pltpu.SemaphoreType.DMA((5,)),
            pltpu.SemaphoreType.DMA((5,)),
            pltpu.SemaphoreType.DMA((9,)),
        ],
        compiler_params=pltpu.CompilerParams(
            collective_id=0, has_side_effects=True, vmem_limit_bytes=32 << 20
        ),
        name="splat_step",
    )(
        *(
            pltpu.with_memory_space_constraint(x, pltpu.HBM)
            for x in (
                seg_count,
                seg_perm,
                params,
                fetch_ids[0].T,
                seg_ids,
                seg_perm.reshape(SEGS, N),
                jnp.transpose(target, (1, 0, 2)),
                moment,
                second,
            )
        )
    )
    image, new_params, new_moment, new_second = pl.pallas_call(
        store,
        out_shape=[shape(x.shape, F32) for x in results],
        in_specs=[vmem] * 4,
        out_specs=[hbm] * 4,
        scratch_shapes=[pltpu.SemaphoreType.DMA((4,))],
        compiler_params=pltpu.CompilerParams(vmem_limit_bytes=1 << 20),
        name="store",
    )(*results)
    return (jnp.transpose(image, (1, 0, 2)), new_params, new_moment, new_second)


def solution(mesh):
    placed = (
        P(None, "dev"),
        P(None, "dev"),
        P(None, "dev"),
        P("dev", None, None),
        P("dev", None),
        P("dev"),
        P(),
        P("dev", None, None),
    )
    return jax.shard_map(
        per_device,
        mesh=mesh,
        in_specs=placed,
        out_specs=(P("dev", None, None), P(None, "dev"), P(None, "dev"), P(None, "dev")),
        check_vma=False,
    )
```
